32 devices in a mesh: slab: 4 (over y, x), energy: 8 (over z, core).
Axes of the slice: x: 2, y: 2, z: 4, core: 2. Of those that a mesh axis runs over, the one named last changes fastest.
Arguments:
- inverse_blocks: float32 [16, 16, 2, 256, 256], P('energy', 'slab'), as said below
- couplings: float32 [16, 16, 2, 256, 256], P('energy', 'slab'), as said below
- lead_column: float32 [16, 2, 256, 256], P('energy'), may hold values from -6 to 6
- w_table: float32 [2, 16383], replicated, may hold values from -1.05 to 1.05
- energy_index: int32 [16], replicated, may hold values from 0 to 8191
Outputs:
- green_column: float32 [16, 16, 2, 256, 256], P('energy', 'slab')
- self_energy: float32 [16, 16, 2, 256, 256], P(None, 'slab', None, 'energy')
The draws below stay inside these ranges and needn't reach their ends.
Inputs may be any that keep to these rules, and one draw needn't show every extreme that they name: `inverse_blocks`: the inverse blocks and couplings each have a diagonal of modulus near 0.95 with random phases and independent off-diagonal entries. `couplings`: as for inverse_blocks, drawn independently.
All inputs are finite; a program needn't handle non-finite values.
Results may differ from the reference program's by a relative error of at most 0.00014.
Values sent between devices are 32-bit elements; how exact they have to be, the bound alone decides.
No kernel may reach another device: no remote copies, remote signals or barrier semaphores. Data moves between devices by JAX's collectives and lax.ppermute only.
A program may use at most 128 MiB of HBM per device.

```python
import math
import jax
import jax.numpy as jnp
from jax import lax

B = 256
GRID = 8192
ENERGIES = 16
NBLK = 16


def block_matrix(key, salt):
    first, second, third = jax.random.split(jax.random.fold_in(key, salt), 3)
    phase = jax.random.uniform(first, (ENERGIES, NBLK, B, 1), jnp.float32, -math.pi, math.pi)
    spread = 0.3 / math.sqrt(2.0 * B)
    off_real = jax.random.normal(second, (ENERGIES, NBLK, B, B), jnp.float32) * spread
    off_imag = jax.random.normal(third, (ENERGIES, NBLK, B, B), jnp.float32) * spread
    rows = jnp.arange(B)[:, None]
    cols = jnp.arange(B)[None, :]
    on_diagonal = rows == cols
    real = jnp.where(on_diagonal, 0.95 * jnp.cos(phase), off_real)
    imag = jnp.where(on_diagonal, 0.95 * jnp.sin(phase), off_imag)
    return jnp.stack([real, imag], axis=2).astype(jnp.float32)


def draw_inverse_blocks(key, part):
    return block_matrix(key, 11)


def draw_couplings(key, part):
    return block_matrix(key, 23)


def with_ends(result, rng, least, largest):
    extent = result.shape
    index_at = [jax.random.randint(jax.random.fold_in(rng, axis), (), 0, extent[axis]) for axis in range(len(extent))]
    result = result.at[tuple(index_at)].set(least)
    longest = extent.index(max(extent))
    index_at[longest] = (index_at[longest] + 1) % extent[longest]
    return result.at[tuple(index_at)].set(largest)


def shard_levels(own_key, shape, pieces, low, high):
    gain = 1.0
    for dim, shards_of in pieces:
        heights = jax.random.uniform(jax.random.fold_in(jax.random.fold_in(own_key, 6), dim), (shards_of,), jnp.float32, low / len(pieces), high / len(pieces))
        gain = gain * jnp.repeat(jnp.exp(heights), shape[dim] // shards_of).reshape((-1,) + (1,) * (len(shape) - 1 - dim))
    return gain


def scatter_about(stream_key, extent, width, bound, cuts=(), held_as=jnp.bfloat16):
    gain = shard_levels(stream_key, extent, cuts, -0.22, 0.18) if cuts else 1.0
    result = jax.random.normal(stream_key, extent, jnp.float32) * width * gain
    return jnp.minimum(jnp.maximum(result, -bound), bound).astype(held_as)


def setup_inputs(seed: int = 0) -> dict:
    splits = jax.random.split(jax.random.key(seed), 6)
    inverse_blocks = draw_inverse_blocks(jax.random.fold_in(splits[5], 71), 0)
    couplings = draw_couplings(jax.random.fold_in(splits[5], 71), 0)
    lead_column = scatter_about(splits[2], (ENERGIES, 2, B, B), 1.0, 6.0, ((0, 8),), jnp.float32)
    w_table = scatter_about(splits[3], (2, 2 * GRID - 1), (0.7 / ENERGIES ** 0.5), 1.05, (), jnp.float32)
    energy_index = with_ends(jax.random.randint(splits[4], (ENERGIES,), 0, GRID), jax.random.fold_in(splits[4], 1), 0, GRID - 1).astype(jnp.int32)
    return dict(inverse_blocks=inverse_blocks, couplings=couplings, lead_column=lead_column, w_table=w_table, energy_index=energy_index)


def complex_product(left, right):
    hp = lax.Precision.HIGHEST
    real = jnp.matmul(left[..., 0, :, :], right[..., 0, :, :], precision=hp) - jnp.matmul(left[..., 1, :, :], right[..., 1, :, :], precision=hp)
    imag = jnp.matmul(left[..., 0, :, :], right[..., 1, :, :], precision=hp) + jnp.matmul(left[..., 1, :, :], right[..., 0, :, :], precision=hp)
    return jnp.stack([real, imag], axis=-3)


def reference(inverse_blocks, couplings, lead_column, w_table, energy_index):
    def advance(carried, pair):
        inverse_one, coupling_one = pair
        transfer = -complex_product(inverse_one, coupling_one)
        nxt = complex_product(transfer, carried)
        return nxt, nxt

    _, columns = lax.scan(advance, lead_column, (jnp.moveaxis(inverse_blocks, 1, 0), jnp.moveaxis(couplings, 1, 0)))
    green_column = jnp.moveaxis(columns, 0, 1)
    offsets = (energy_index[:, None] - energy_index[None, :] + GRID - 1).astype(jnp.int32)
    kernel_real = w_table[0][offsets]
    kernel_imag = w_table[1][offsets]
    count = green_column.shape[0]
    flat_real = green_column[:, :, 0].reshape(count, -1)
    flat_imag = green_column[:, :, 1].reshape(count, -1)
    hp = lax.Precision.HIGHEST
    out_real = jnp.dot(kernel_real, flat_real, precision=hp) - jnp.dot(kernel_imag, flat_imag, precision=hp)
    out_imag = jnp.dot(kernel_real, flat_imag, precision=hp) + jnp.dot(kernel_imag, flat_real, precision=hp)
    shape = green_column[:, :, 0].shape
    self_energy = jnp.stack([out_real.reshape(shape), out_imag.reshape(shape)], axis=2)
    return green_column, self_energy
```

```python
import functools

import jax
import jax.numpy as jnp
from jax import lax
from jax.experimental import pallas as pl
from jax.experimental.pallas import tpu as pltpu
from jax.sharding import PartitionSpec as P


F32 = jnp.float32
BF16 = jnp.bfloat16
SUBLANES = 8


def split(x):
    high = x.astype(BF16)
    return high, (x - high.astype(F32)).astype(BF16)


def dot3(left, right):
    def dot(a, b):
        return jnp.dot(a, b, preferred_element_type=F32)

    return dot(left[0], right[0]) + (dot(left[0], right[1]) + dot(left[1], right[0]))


def left_parts(real, imag):
    return split(real + imag), split(real), split(imag)


def right_parts(real, imag):
    return split(real), split(imag - real), split(real + imag)


def complex_product(left, right):
    first = dot3(left[0], right[0])
    second = dot3(left[1], right[1])
    third = dot3(left[2], right[2])
    return first - third, first + second


def prefix_kernel(g_ref, h_ref, p_ref, q_ref):
    block = pl.program_id(0)
    real, imag = complex_product(
        left_parts(g_ref[0, 0, 0], g_ref[0, 0, 1]), right_parts(h_ref[0, 0, 0], h_ref[0, 0, 1])
    )
    real, imag = -real, -imag

    @pl.when(block == 0)
    def _():
        q_ref[0] = real
        q_ref[1] = imag

    @pl.when(block > 0)
    def _():
        re, im = complex_product(left_parts(real, imag), right_parts(q_ref[0], q_ref[1]))
        q_ref[0] = re
        q_ref[1] = im

    p_ref[0] = q_ref[...]


def prefixes(inverse_blocks, couplings, energy):
    _, blocks, _, size, _ = inverse_blocks.shape
    spec = pl.BlockSpec((1, 1, 2, size, size), lambda k: (energy, k, 0, 0, 0))
    return pl.pallas_call(
        prefix_kernel,
        grid=(blocks,),
        in_specs=[spec, spec],
        out_specs=[
            pl.BlockSpec((1, 2, size, size), lambda k: (k, 0, 0, 0)),
            pl.BlockSpec((2, size, size), lambda k: (0, 0, 0)),
        ],
        out_shape=[
            jax.ShapeDtypeStruct((blocks, 2, size, size), F32),
            jax.ShapeDtypeStruct((2, size, size), F32),
        ],
        name="prefixes",
    )(inverse_blocks, couplings)


def column_kernel(n_slabs, rows, *refs):
    position, p_ref = refs[0], refs[1]
    arrived = refs[2 : 1 + n_slabs]
    lead_ref = refs[1 + n_slabs]
    green_ref, send_ref, carried = refs[-3:]

    @pl.when(pl.program_id(0) == 0)
    def _():
        carried[...] = lead_ref[0]
        for distance in range(n_slabs - 1, 0, -1):

            @pl.when(position[0] >= distance)
            def _():
                ref = arrived[distance - 1]
                re, im = complex_product(
                    left_parts(ref[0], ref[1]), right_parts(carried[0], carried[1])
                )
                carried[0] = re
                carried[1] = im

    re, im = complex_product(
        left_parts(p_ref[0, 0], p_ref[0, 1]), right_parts(carried[0], carried[1])
    )
    for part, value in enumerate((re, im)):
        green_ref[0, 0, part] = value
        send_ref[:, 0, part] = value.reshape(-1, rows, value.shape[-1])


def columns(position, prefix, arrived, lead, energy, n_energy, green_before):
    blocks, _, size, _ = prefix.shape
    energies = lead.shape[0]
    rows = size // n_energy
    n_slabs = len(arrived) + 1
    whole = pl.BlockSpec((2, size, size), lambda k, s: (0, 0, 0))
    in_specs = [
        pl.BlockSpec((1, 2, size, size), lambda k, s: (k, 0, 0, 0)),
        *[whole] * len(arrived),
        pl.BlockSpec((1, 2, size, size), lambda k, s: (energy, 0, 0, 0)),
    ]
    operands = [prefix, *arrived, lead]
    aliases = {}
    kernel = functools.partial(column_kernel, n_slabs, rows)
    if green_before is not None:
        in_specs.append(pl.BlockSpec(memory_space=pl.ANY))
        operands.append(green_before)
        aliases = {len(operands): 0}
    return pl.pallas_call(
        kernel,
        grid_spec=pltpu.PrefetchScalarGridSpec(
            num_scalar_prefetch=1,
            grid=(blocks,),
            in_specs=in_specs,
            out_specs=[
                pl.BlockSpec((1, 1, 2, size, size), lambda k, s: (energy, k, 0, 0, 0)),
                pl.BlockSpec((n_energy, 1, 2, rows, size), lambda k, s: (0, k, 0, 0, 0)),
            ],
            scratch_shapes=[pltpu.VMEM((2, size, size), F32)],
        ),
        out_shape=[
            jax.ShapeDtypeStruct((energies, blocks, 2, size, size), F32),
            jax.ShapeDtypeStruct((n_energy, blocks, 2, rows, size), F32),
        ],
        input_output_aliases=aliases,
        name="columns",
    )(position, *operands)


def mixing_matrix(energy_index, w_table, local, n_energy):
    grid_points = (w_table.shape[1] + 1) // 2
    order = jnp.arange(n_energy * local).reshape(n_energy, local).T.reshape(-1)
    offsets = energy_index[:, None] - energy_index[order][None, :] + grid_points - 1
    real = w_table[0][offsets]
    imag = w_table[1][offsets]
    pairs = jnp.stack([jnp.stack([real, -imag], -1), jnp.stack([imag, real], -1)], 1)
    spread = pairs[:, :, None, :, :, None] * jnp.eye(SUBLANES, dtype=F32)[:, None, None, :]
    count = energy_index.shape[0] * 2 * SUBLANES
    return spread.reshape(count, count)


def convolve_kernel(*refs):
    mix_ref = refs[0]
    gathered = refs[1:-3]
    out_ref, high, low = refs[-3:]
    rows, lanes = out_ref.shape[-2:]

    @pl.when(pl.program_id(0) == 0)
    def _():
        h, l = split(mix_ref[...])
        high[...] = h
        low[...] = l

    for start in range(0, rows, SUBLANES):
        piece = jnp.concatenate(
            [ref[:, 0, :, start : start + SUBLANES, :].reshape(-1, lanes) for ref in gathered], 0
        )
        mixed = dot3((high[...], low[...]), split(piece))
        out_ref[:, 0, :, start : start + SUBLANES, :] = mixed.reshape(-1, 2, SUBLANES, lanes)


def convolve(mix, gathered):
    n_energy, blocks, _, rows, size = gathered[0].shape
    count = mix.shape[0]
    energies = n_energy * len(gathered)
    return pl.pallas_call(
        convolve_kernel,
        grid=(blocks,),
        in_specs=[
            pl.BlockSpec((count, count), lambda k: (0, 0)),
            *[pl.BlockSpec((n_energy, 1, 2, rows, size), lambda k: (0, k, 0, 0, 0))] * len(gathered),
        ],
        out_specs=pl.BlockSpec((energies, 1, 2, rows, size), lambda k: (0, k, 0, 0, 0)),
        out_shape=jax.ShapeDtypeStruct((energies, blocks, 2, rows, size), F32),
        scratch_shapes=[pltpu.VMEM((count, count), BF16), pltpu.VMEM((count, count), BF16)],
        name="convolve",
    )(mix, *gathered)


def per_device(inverse_blocks, couplings, lead_column, w_table, energy_index):
    n_slabs = lax.axis_size("slab")
    n_energy = lax.axis_size("energy")
    local = inverse_blocks.shape[0]
    position = lax.axis_index("slab").reshape(1).astype(jnp.int32)
    prefix, arrived = [], []
    for energy in range(local):
        p, last = prefixes(inverse_blocks, couplings, energy)
        prefix.append(p)
        arrived.append(
            [
                lax.ppermute(last, "slab", [(i, i + d) for i in range(n_slabs - d)])
                for d in range(1, n_slabs)
            ]
        )
    mix = mixing_matrix(energy_index, w_table, local, n_energy)
    green, gathered = None, []
    for energy in range(local):
        green, send = columns(
            position, prefix[energy], arrived[energy], lead_column, energy, n_energy, green
        )
        gathered.append(lax.all_to_all(send, "energy", 0, 0, tiled=True))
    return green, convolve(mix, gathered)


def solution(mesh):
    placed = (
        P("energy", "slab", None, None, None),
        P("energy", "slab", None, None, None),
        P("energy", None, None, None),
        P(),
        P(),
    )
    return jax.shard_map(
        per_device,
        mesh=mesh,
        in_specs=placed,
        out_specs=(P("energy", "slab", None, None, None), P(None, "slab", None, "energy", None)),
        check_vma=False,
    )
```

```python
import functools

import jax
import jax.numpy as jnp
from jax import lax
from jax.experimental import pallas as pl
from jax.experimental.pallas import tpu as pltpu
from jax.sharding import PartitionSpec as P


F32 = jnp.float32
BF16 = jnp.bfloat16
SUBLANES = 8
LANES = 128
VMEM_LIMIT = 24 * 2**20


def split(x):
    high = x.astype(BF16)
    return high, (x - high.astype(F32)).astype(BF16)


def dot3(left, right):
    def dot(a, b):
        return jnp.dot(a, b, preferred_element_type=F32)

    return dot(left[0], right[0]) + (dot(left[0], right[1]) + dot(left[1], right[0]))


def left_parts(real, imag):
    return split(real + imag), split(real), split(imag)


def right_parts(real, imag):
    return split(real), split(imag - real), split(real + imag)


def complex_product(left, right):
    first = dot3(left[0], right[0])
    second = dot3(left[1], right[1])
    third = dot3(left[2], right[2])
    return first - third, first + second


def compiler_params():
    return pltpu.CompilerParams(vmem_limit_bytes=VMEM_LIMIT)


def prefix_kernel(position, g_ref, h_ref, lead_ref, p_ref, q_ref, *first_refs):
    block = pl.program_id(0)
    real, imag = complex_product(
        left_parts(g_ref[0, 0, 0], g_ref[0, 0, 1]), right_parts(h_ref[0, 0, 0], h_ref[0, 0, 1])
    )
    real, imag = -real, -imag

    @pl.when(block == 0)
    def _():
        q_ref[0] = real
        q_ref[1] = imag

    @pl.when(block > 0)
    def _():
        re, im = complex_product(left_parts(real, imag), right_parts(q_ref[0], q_ref[1]))
        q_ref[0] = re
        q_ref[1] = im

    p_ref[0] = q_ref[...]

    @pl.when((block == pl.num_programs(0) - 1) & (position[0] == 0))
    def _():
        re, im = complex_product(
            left_parts(q_ref[0], q_ref[1]), right_parts(lead_ref[0, 0], lead_ref[0, 1])
        )
        for i, ref in enumerate(first_refs):
            width = ref.shape[-1]
            ref[0] = re[:, i * width : (i + 1) * width]
            ref[1] = im[:, i * width : (i + 1) * width]


def prefixes(position, inverse_blocks, couplings, lead, energy, strips):
    _, blocks, _, size, _ = inverse_blocks.shape
    width = size // strips
    spec = pl.BlockSpec((1, 1, 2, size, size), lambda k, s: (energy, k, 0, 0, 0))
    whole = lambda width: pl.BlockSpec((2, size, width), lambda k, s: (0, 0, 0))
    return pl.pallas_call(
        prefix_kernel,
        grid_spec=pltpu.PrefetchScalarGridSpec(
            num_scalar_prefetch=1,
            grid=(blocks,),
            in_specs=[
                spec,
                spec,
                pl.BlockSpec((1, 2, size, size), lambda k, s: (energy, 0, 0, 0)),
            ],
            out_specs=[
                pl.BlockSpec((1, 2, size, size), lambda k, s: (k, 0, 0, 0)),
                whole(size),
                *[whole(width)] * strips,
            ],
        ),
        out_shape=[
            jax.ShapeDtypeStruct((blocks, 2, size, size), F32),
            jax.ShapeDtypeStruct((2, size, size), F32),
            *[jax.ShapeDtypeStruct((2, size, width), F32)] * strips,
        ],
        compiler_params=compiler_params(),
        name="prefixes",
    )(position, inverse_blocks, couplings, lead)


def column_kernel(n_slabs, n_energy, strip, *refs):
    position, p_ref, lead_ref = refs[:3]
    products = refs[3 : 1 + n_slabs]
    firsts = refs[1 + n_slabs : 2 * n_slabs]
    sends = refs[-1 - n_energy : -1]
    green_ref, carried = refs[-2 - n_energy], refs[-1]
    rows, lanes = sends[0].shape[-2:]

    @pl.when(pl.program_id(0) == 0)
    def _():
        @pl.when(position[0] == 0)
        def _():
            carried[...] = lead_ref[0, :, :, strip * lanes : (strip + 1) * lanes]

        for distance in range(1, n_slabs):

            @pl.when(position[0] == distance)
            def _():
                carried[...] = firsts[distance - 1][...]

        for distance in range(n_slabs - 2, 0, -1):

            @pl.when(position[0] > distance)
            def _():
                ref = products[distance - 1]
                re, im = complex_product(
                    left_parts(ref[0], ref[1]), right_parts(carried[0], carried[1])
                )
                carried[0] = re
                carried[1] = im

    re, im = complex_product(
        left_parts(p_ref[0, 0], p_ref[0, 1]), right_parts(carried[0], carried[1])
    )
    for part, value in enumerate((re, im)):
        green_ref[0, 0, part] = value
    for step, send in enumerate(sends):
        start = pl.multiple_of(partner(position[1], step, n_energy) * rows, rows)
        send[0] = green_ref[0, 0, :, pl.ds(start, rows), :]


def partner(me, step, count):
    if count & (count - 1) == 0:
        return me ^ step
    return (me + step) % count


def columns(position, prefix, lead, products, firsts, energy, strip, n_energy, before):
    blocks, _, size, _ = prefix.shape
    energies = lead.shape[0]
    rows = size // n_energy
    lanes = firsts[0].shape[-1] if firsts else LANES
    n_slabs = len(firsts) + 1
    square = pl.BlockSpec((2, size, size), lambda k, s: (0, 0, 0))
    narrow = pl.BlockSpec((2, size, lanes), lambda k, s: (0, 0, 0))
    in_specs = [
        pl.BlockSpec((1, 2, size, size), lambda k, s: (k, 0, 0, 0)),
        pl.BlockSpec((1, 2, size, size), lambda k, s: (energy, 0, 0, 0)),
        *[square] * len(products),
        *[narrow] * len(firsts),
    ]
    operands = [prefix, lead, *products, *firsts]
    aliases = {}
    if before is not None:
        in_specs.append(pl.BlockSpec(memory_space=pl.ANY))
        operands.append(before)
        aliases = {len(operands): 0}
    green, *sends = pl.pallas_call(
        functools.partial(column_kernel, n_slabs, n_energy, strip),
        grid_spec=pltpu.PrefetchScalarGridSpec(
            num_scalar_prefetch=1,
            grid=(blocks,),
            in_specs=in_specs,
            out_specs=[
                pl.BlockSpec((1, 1, 2, size, lanes), lambda k, s: (energy, k, 0, 0, strip)),
                *[pl.BlockSpec((1, 2, rows, lanes), lambda k, s: (k, 0, 0, 0))] * n_energy,
            ],
            scratch_shapes=[pltpu.VMEM((2, size, lanes), F32)],
        ),
        out_shape=[
            jax.ShapeDtypeStruct((energies, blocks, 2, size, size), F32),
            *[jax.ShapeDtypeStruct((blocks, 2, rows, lanes), F32)] * n_energy,
        ],
        input_output_aliases=aliases,
        compiler_params=compiler_params(),
        name="columns",
    )(position, *operands)
    return green, sends


def spread_kernel(real_ref, imag_ref, high_ref, low_ref):
    energies = real_ref.shape[0]
    count = high_ref.shape[0]
    group = count // energies
    row = lax.broadcasted_iota(jnp.int32, (count, energies), 0) // group
    to_row = (row == lax.broadcasted_iota(jnp.int32, (count, energies), 1)).astype(BF16)
    column = lax.broadcasted_iota(jnp.int32, (energies, count), 1) // group
    to_column = (column == lax.broadcasted_iota(jnp.int32, (energies, count), 0)).astype(BF16)
    rows = lax.broadcasted_iota(jnp.int32, (count, count), 0) % group
    columns = lax.broadcasted_iota(jnp.int32, (count, count), 1) % group
    same_part = rows == columns
    below = rows == columns + SUBLANES
    above = rows + SUBLANES == columns

    def spread(x):
        tall = jnp.dot(to_row, x, preferred_element_type=F32).astype(BF16)
        return jnp.dot(tall, to_column, preferred_element_type=F32)

    for out, real, imag in zip(
        (high_ref, low_ref), split(real_ref[...]), split(imag_ref[...]), strict=True
    ):
        re, im = spread(real), spread(imag)
        out[...] = jnp.where(
            same_part, re, jnp.where(below, im, jnp.where(above, -im, 0.0))
        ).astype(BF16)


def mixing_matrix(energy_index, w_table, local, n_energy):
    grid_points = (w_table.shape[1] + 1) // 2
    energies = energy_index.shape[0]
    sources = partner(lax.axis_index("energy"), jnp.arange(n_energy), n_energy)
    column = energy_index.reshape(n_energy, local)[sources].T.reshape(-1)
    offsets = energy_index[:, None] - column[None, :] + grid_points - 1
    count = energies * 2 * SUBLANES
    return pl.pallas_call(
        spread_kernel,
        out_shape=[jax.ShapeDtypeStruct((count, count), BF16)] * 2,
        compiler_params=compiler_params(),
        name="spread",
    )(w_table[0][offsets], w_table[1][offsets])


def convolve_kernel(count, high_ref, low_ref, *refs):
    gathered, out_ref = refs[:count], refs[-1]
    rows, lanes = out_ref.shape[-2:]
    piece = jnp.concatenate(
        [
            jnp.concatenate(
                [
                    ref[0, :, start : start + SUBLANES, :].reshape(-1, lanes)
                    for start in range(0, rows, SUBLANES)
                ],
                1,
            )
            for ref in gathered
        ],
        0,
    )
    mixed = dot3((high_ref[...], low_ref[...]), split(piece))
    for i, start in enumerate(range(0, rows, SUBLANES)):
        out_ref[:, 0, :, start : start + SUBLANES, :] = mixed[
            :, i * lanes : (i + 1) * lanes
        ].reshape(-1, 2, SUBLANES, lanes)


def convolve(mix, gathered, strip, strips, before):
    blocks, _, rows, lanes = gathered[0].shape
    count = mix[0].shape[0]
    energies = len(gathered)
    matrix = pl.BlockSpec((count, count), lambda k: (0, 0))
    piece = pl.BlockSpec((1, 2, rows, lanes), lambda k: (k, 0, 0, 0))
    in_specs = [matrix, matrix, *[piece] * energies]
    operands = [*mix, *gathered]
    aliases = {}
    if before is not None:
        in_specs.append(pl.BlockSpec(memory_space=pl.ANY))
        operands.append(before)
        aliases = {len(operands) - 1: 0}
    return pl.pallas_call(
        functools.partial(convolve_kernel, energies),
        grid=(blocks,),
        in_specs=in_specs,
        out_specs=pl.BlockSpec((energies, 1, 2, rows, lanes), lambda k: (0, k, 0, 0, strip)),
        out_shape=jax.ShapeDtypeStruct((energies, blocks, 2, rows, strips * lanes), F32),
        input_output_aliases=aliases,
        compiler_params=compiler_params(),
        name="convolve",
    )(*operands)


def per_device(inverse_blocks, couplings, lead_column, w_table, energy_index):
    n_slabs = lax.axis_size("slab")
    n_energy = lax.axis_size("energy")
    local = inverse_blocks.shape[0]
    strips = inverse_blocks.shape[-1] // LANES
    position = jnp.stack([lax.axis_index("slab"), lax.axis_index("energy")]).astype(jnp.int32)
    prefix, products, firsts = [], [], []
    for e in range(local):
        p, last, *first = prefixes(position, inverse_blocks, couplings, lead_column, e, strips)
        prefix.append(p)
        products.append(
            [
                lax.ppermute(last, "slab", [(i, i + d) for i in range(1, n_slabs - d)])
                for d in range(1, n_slabs - 1)
            ]
        )
        firsts.append(
            [[lax.ppermute(one, "slab", [(0, d)]) for d in range(1, n_slabs)] for one in first]
        )
    mix = mixing_matrix(energy_index, w_table, local, n_energy)
    green = None
    gathered = [[None] * (local * n_energy) for _ in range(strips)]
    for e in range(local):
        for strip in range(strips):
            green, sends = columns(
                position,
                prefix[e],
                lead_column,
                products[e],
                firsts[e][strip],
                e,
                strip,
                n_energy,
                green,
            )
            for step in sorted(range(n_energy), reverse=True):
                received = sends[step]
                if step:
                    route = [(i, partner(i, step, n_energy)) for i in range(n_energy)]
                    received = lax.ppermute(received, "energy", route)
                gathered[strip][e * n_energy + step] = received
    mixed = None
    for strip in range(strips):
        mixed = convolve(mix, gathered[strip], strip, strips, mixed)
    return green, mixed


def solution(mesh):
    placed = (
        P("energy", "slab", None, None, None),
        P("energy", "slab", None, None, None),
        P("energy", None, None, None),
        P(),
        P(),
    )
    return jax.shard_map(
        per_device,
        mesh=mesh,
        in_specs=placed,
        out_specs=(P("energy", "slab", None, None, None), P(None, "slab", None, "energy", None)),
        check_vma=False,
    )
```

```python
import functools

import jax
import jax.numpy as jnp
from jax import lax
from jax.experimental import pallas as pl
from jax.experimental.pallas import tpu as pltpu
from jax.sharding import PartitionSpec as P


F32 = jnp.float32
BF16 = jnp.bfloat16
SUBLANES = 8
LANES = 128
VMEM_LIMIT = 24 * 2**20


def split(x):
    high = x.astype(BF16)
    return high, (x - high.astype(F32)).astype(BF16)


def dot3(left, right):
    def dot(a, b):
        return jnp.dot(a, b, preferred_element_type=F32)

    return dot(left[0], right[0]) + (dot(left[0], right[1]) + dot(left[1], right[0]))


def left_parts(real, imag):
    return split(real + imag), split(real), split(imag)


def right_parts(real, imag):
    return split(real), split(imag - real), split(real + imag)


def complex_product(left, right):
    first = dot3(left[0], right[0])
    second = dot3(left[1], right[1])
    third = dot3(left[2], right[2])
    return first - third, first + second


def compiler_params():
    return pltpu.CompilerParams(vmem_limit_bytes=VMEM_LIMIT)


def prefix_kernel(position, g_ref, h_ref, lead_ref, p_ref, q_ref, *first_refs):
    block = pl.program_id(0)
    real, imag = complex_product(
        left_parts(g_ref[0, 0, 0], g_ref[0, 0, 1]), right_parts(h_ref[0, 0, 0], h_ref[0, 0, 1])
    )
    real, imag = -real, -imag

    @pl.when(block == 0)
    def _():
        q_ref[0] = real
        q_ref[1] = imag

    @pl.when(block > 0)
    def _():
        re, im = complex_product(left_parts(real, imag), right_parts(q_ref[0], q_ref[1]))
        q_ref[0] = re
        q_ref[1] = im

    p_ref[0] = q_ref[...]

    @pl.when((block == pl.num_programs(0) - 1) & (position[0] == 0))
    def _():
        re, im = complex_product(
            left_parts(q_ref[0], q_ref[1]), right_parts(lead_ref[0, 0], lead_ref[0, 1])
        )
        for i, ref in enumerate(first_refs):
            width = ref.shape[-1]
            ref[0] = re[:, i * width : (i + 1) * width]
            ref[1] = im[:, i * width : (i + 1) * width]


def prefixes(position, inverse_blocks, couplings, lead, energy, strips):
    _, blocks, _, size, _ = inverse_blocks.shape
    width = size // strips
    spec = pl.BlockSpec((1, 1, 2, size, size), lambda k, s: (energy, k, 0, 0, 0))
    whole = lambda width: pl.BlockSpec((2, size, width), lambda k, s: (0, 0, 0))
    return pl.pallas_call(
        prefix_kernel,
        grid_spec=pltpu.PrefetchScalarGridSpec(
            num_scalar_prefetch=1,
            grid=(blocks,),
            in_specs=[
                spec,
                spec,
                pl.BlockSpec((1, 2, size, size), lambda k, s: (energy, 0, 0, 0)),
            ],
            out_specs=[
                pl.BlockSpec((1, 2, size, size), lambda k, s: (k, 0, 0, 0)),
                whole(size),
                *[whole(width)] * strips,
            ],
        ),
        out_shape=[
            jax.ShapeDtypeStruct((blocks, 2, size, size), F32),
            jax.ShapeDtypeStruct((2, size, size), F32),
            *[jax.ShapeDtypeStruct((2, size, width), F32)] * strips,
        ],
        name="prefixes",
    )(position, inverse_blocks, couplings, lead)


def column_kernel(n_slabs, n_energy, strip, *refs):
    position, p_ref, lead_ref = refs[:3]
    products = refs[3 : 1 + n_slabs]
    firsts = refs[1 + n_slabs : 2 * n_slabs]
    sends = refs[-1 - n_energy : -1]
    green_ref, carried = refs[-2 - n_energy], refs[-1]
    rows, lanes = sends[0].shape[-2:]
    columns = slice(strip * lanes, (strip + 1) * lanes)

    @pl.when(pl.program_id(0) == 0)
    def _():
        @pl.when(position[0] == 0)
        def _():
            carried[...] = lead_ref[0, :, :, columns]

        for distance in range(1, n_slabs):

            @pl.when(position[0] == distance)
            def _():
                ref = firsts[distance - 1]
                carried[...] = ref[...] if ref.shape[-1] == lanes else ref[:, :, columns]

        for distance in range(n_slabs - 2, 0, -1):

            @pl.when(position[0] > distance)
            def _():
                ref = products[distance - 1]
                re, im = complex_product(
                    left_parts(ref[0], ref[1]), right_parts(carried[0], carried[1])
                )
                carried[0] = re
                carried[1] = im

    re, im = complex_product(
        left_parts(p_ref[0, 0], p_ref[0, 1]), right_parts(carried[0], carried[1])
    )
    for part, value in enumerate((re, im)):
        green_ref[0, 0, part] = value
    for step, send in enumerate(sends):
        start = pl.multiple_of(partner(position[1], step, n_energy) * rows, rows)
        send[0] = green_ref[0, 0, :, pl.ds(start, rows), :]


def partner(me, step, count):
    if count & (count - 1) == 0:
        return me ^ step
    return (me + step) % count


def columns(position, prefix, lead, products, firsts, energy, strip, n_energy, before):
    blocks, _, size, _ = prefix.shape
    energies = lead.shape[0]
    rows = size // n_energy
    lanes = LANES
    n_slabs = len(firsts) + 1
    square = pl.BlockSpec((2, size, size), lambda k, s: (0, 0, 0))
    in_specs = [
        pl.BlockSpec((1, 2, size, size), lambda k, s: (k, 0, 0, 0)),
        pl.BlockSpec((1, 2, size, size), lambda k, s: (energy, 0, 0, 0)),
        *[square] * len(products),
        *[pl.BlockSpec(first.shape, lambda k, s: (0, 0, 0)) for first in firsts],
    ]
    operands = [prefix, lead, *products, *firsts]
    aliases = {}
    if before is not None:
        in_specs.append(pl.BlockSpec(memory_space=pl.ANY))
        operands.append(before)
        aliases = {len(operands): 0}
    green, *sends = pl.pallas_call(
        functools.partial(column_kernel, n_slabs, n_energy, strip),
        grid_spec=pltpu.PrefetchScalarGridSpec(
            num_scalar_prefetch=1,
            grid=(blocks,),
            in_specs=in_specs,
            out_specs=[
                pl.BlockSpec((1, 1, 2, size, lanes), lambda k, s: (energy, k, 0, 0, strip)),
                *[pl.BlockSpec((1, 2, rows, lanes), lambda k, s: (k, 0, 0, 0))] * n_energy,
            ],
            scratch_shapes=[pltpu.VMEM((2, size, lanes), F32)],
        ),
        out_shape=[
            jax.ShapeDtypeStruct((energies, blocks, 2, size, size), F32),
            *[jax.ShapeDtypeStruct((blocks, 2, rows, lanes), F32)] * n_energy,
        ],
        input_output_aliases=aliases,
        compiler_params=compiler_params(),
        name="columns",
    )(position, *operands)
    return green, sends


def spread_kernel(real_ref, imag_ref, high_ref, low_ref):
    energies = real_ref.shape[0]
    count = high_ref.shape[0]
    group = count // energies
    row = lax.broadcasted_iota(jnp.int32, (count, energies), 0) // group
    to_row = (row == lax.broadcasted_iota(jnp.int32, (count, energies), 1)).astype(BF16)
    column = lax.broadcasted_iota(jnp.int32, (energies, count), 1) // group
    to_column = (column == lax.broadcasted_iota(jnp.int32, (energies, count), 0)).astype(BF16)
    rows = lax.broadcasted_iota(jnp.int32, (count, count), 0) % group
    columns = lax.broadcasted_iota(jnp.int32, (count, count), 1) % group
    same_part = rows == columns
    below = rows == columns + SUBLANES
    above = rows + SUBLANES == columns

    def spread(x):
        tall = jnp.dot(to_row, x, preferred_element_type=F32).astype(BF16)
        return jnp.dot(tall, to_column, preferred_element_type=F32)

    for out, real, imag in zip(
        (high_ref, low_ref), split(real_ref[...]), split(imag_ref[...]), strict=True
    ):
        re, im = spread(real), spread(imag)
        out[...] = jnp.where(
            same_part, re, jnp.where(below, im, jnp.where(above, -im, 0.0))
        ).astype(BF16)


def mixing_matrix(energy_index, w_table, local, n_energy):
    grid_points = (w_table.shape[1] + 1) // 2
    energies = energy_index.shape[0]
    sources = partner(lax.axis_index("energy"), jnp.arange(n_energy), n_energy)
    column = energy_index.reshape(n_energy, local)[sources].T.reshape(-1)
    offsets = energy_index[:, None] - column[None, :] + grid_points - 1
    count = energies * 2 * SUBLANES
    return pl.pallas_call(
        spread_kernel,
        out_shape=[jax.ShapeDtypeStruct((count, count), BF16)] * 2,
        compiler_params=compiler_params(),
        name="spread",
    )(w_table[0][offsets], w_table[1][offsets])


def convolve_kernel(count, high_ref, low_ref, *refs):
    gathered, out_ref = refs[:count], refs[-1]
    rows, lanes = out_ref.shape[-2:]
    piece = jnp.concatenate(
        [
            jnp.concatenate(
                [
                    ref[0, :, start : start + SUBLANES, :].reshape(-1, lanes)
                    for start in range(0, rows, SUBLANES)
                ],
                1,
            )
            for ref in gathered
        ],
        0,
    )
    mixed = dot3((high_ref[...], low_ref[...]), split(piece))
    for i, start in enumerate(range(0, rows, SUBLANES)):
        out_ref[:, 0, :, start : start + SUBLANES, :] = mixed[
            :, i * lanes : (i + 1) * lanes
        ].reshape(-1, 2, SUBLANES, lanes)


def convolve(mix, gathered, strip, strips, before):
    blocks, _, rows, lanes = gathered[0].shape
    count = mix[0].shape[0]
    energies = len(gathered)
    matrix = pl.BlockSpec((count, count), lambda k: (0, 0))
    piece = pl.BlockSpec((1, 2, rows, lanes), lambda k: (k, 0, 0, 0))
    in_specs = [matrix, matrix, *[piece] * energies]
    operands = [*mix, *gathered]
    aliases = {}
    if before is not None:
        in_specs.append(pl.BlockSpec(memory_space=pl.ANY))
        operands.append(before)
        aliases = {len(operands) - 1: 0}
    return pl.pallas_call(
        functools.partial(convolve_kernel, energies),
        grid=(blocks,),
        in_specs=in_specs,
        out_specs=pl.BlockSpec((energies, 1, 2, rows, lanes), lambda k: (0, k, 0, 0, strip)),
        out_shape=jax.ShapeDtypeStruct((energies, blocks, 2, rows, strips * lanes), F32),
        input_output_aliases=aliases,
        compiler_params=compiler_params(),
        name="convolve",
    )(*operands)


def per_device(inverse_blocks, couplings, lead_column, w_table, energy_index):
    n_slabs = lax.axis_size("slab")
    n_energy = lax.axis_size("energy")
    local = inverse_blocks.shape[0]
    strips = inverse_blocks.shape[-1] // LANES
    position = jnp.stack([lax.axis_index("slab"), lax.axis_index("energy")]).astype(jnp.int32)
    prefix, products, firsts = [], [], []
    for e in range(local):
        p, last, *first = prefixes(
            position, inverse_blocks, couplings, lead_column, e, 1 if e else strips
        )
        prefix.append(p)
        products.append(
            [
                lax.ppermute(last, "slab", [(i, i + d) for i in range(1, n_slabs - d)])
                for d in range(1, n_slabs - 1)
            ]
        )
        firsts.append([])
        for one in first:
            firsts[e].append([lax.ppermute(one, "slab", [(0, d)]) for d in range(1, n_slabs)])
    mix = mixing_matrix(energy_index, w_table, local, n_energy)
    green = None
    gathered = [[None] * (local * n_energy) for _ in range(strips)]
    for e in range(local):
        for strip in range(strips):
            green, sends = columns(
                position,
                prefix[e],
                lead_column,
                products[e],
                firsts[e][min(strip, len(firsts[e]) - 1)],
                e,
                strip,
                n_energy,
                green,
            )
            for step in sorted(range(n_energy), reverse=True):
                received = sends[step]
                if step:
                    route = [(i, partner(i, step, n_energy)) for i in range(n_energy)]
                    received = lax.ppermute(received, "energy", route)
                gathered[strip][e * n_energy + step] = received
    mixed = None
    for strip in range(strips):
        mixed = convolve(mix, gathered[strip], strip, strips, mixed)
    return green, mixed


def solution(mesh):
    placed = (
        P("energy", "slab", None, None, None),
        P("energy", "slab", None, None, None),
        P("energy", None, None, None),
        P(),
        P(),
    )
    return jax.shard_map(
        per_device,
        mesh=mesh,
        in_specs=placed,
        out_specs=(P("energy", "slab", None, None, None), P(None, "slab", None, "energy", None)),
        check_vma=False,
    )
```
